32 devices in a mesh: gx: 4 (over y, x), gy: 8 (over z, core).
Axes of the slice: x: 2, y: 2, z: 4, core: 2. Of those that a mesh axis runs over, the one named last changes fastest.
Arguments:
- density: float32 [32, 32, 128], P('gx', 'gy'), may hold values from -5 to 5
- susceptibility: float32 [32, 32, 128], P('gx', 'gy'), may hold values from -5 to 5
- station_cell: int32 [2, 1024], P(None, 'gx'), may hold values from 0 to 1023
- station_line: int32 [2, 1024], P(None, 'gx'), may hold values from 0 to 255, as said below
- observed: float32 [2, 1024], P(None, 'gx'), may hold values from -3 to 3
- data_weight: float32 [2, 1024], P(None, 'gx'), may hold values from 0.5 to 2
- trial_steps: float32 [8], replicated, may hold values from 0.05 to 0.5
Outputs:
- data_gradient: float32 [2, 32, 32, 128], P(None, 'gx', 'gy')
- cross_force: float32 [2, 32, 32, 128], P(None, 'gx', 'gy')
- weighted_residual: float32 [2, 1024], P(None, 'gx')
- trial_values: float32 [8], replicated
The draws below stay inside these ranges and needn't reach their ends.
Inputs may be any that keep to these rules, and one draw needn't show every extreme that they name: `station_line`: one or more survey lines hold no station of either field.
All inputs are finite; a program needn't handle non-finite values. Where the reference program divides by a largest or mean magnitude, that divisor is 1e-20 or more.
Results may differ from the reference program's by a relative error of at most 0.0003.
Values sent between devices are 32-bit elements; how exact they have to be, the bound alone decides.
No kernel may reach another device: no remote copies, remote signals or barrier semaphores. Data moves between devices by JAX's collectives and lax.ppermute only.
A program may use at most 64 MiB of HBM per device.

```python
import math
import jax
import jax.numpy as jnp
from jax import lax

NZ = 128
LINES = 256
TRIALS = 8
NX = 32
NY = 32
STATIONS = 1024


def draw_density(key, part):
    return jnp.clip(jax.random.normal(key, (NX, NY, NZ), jnp.float32), -5.0, 5.0)


def draw_susceptibility(key, part):
    inner = jax.random.fold_in(key, 7)
    return jnp.clip(jax.random.normal(inner, (NX, NY, NZ), jnp.float32), -5.0, 5.0)


def draw_station_line(key, part):
    table_key = jax.random.fold_in(key, 11)
    pick_key = jax.random.fold_in(key, 12)
    missing_key = jax.random.fold_in(key, 13)
    table = jax.random.randint(table_key, (LINES,), 0, LINES, jnp.int32)
    missing = jax.random.randint(missing_key, (), 0, LINES, jnp.int32)
    table = jnp.where(table == missing, (table + 1) % LINES, table)
    picks = jax.random.randint(pick_key, (2, STATIONS), 0, LINES, jnp.int32)
    return table[picks]


def with_ends(result, key, least, high):
    longest = result.shape.index(max(result.shape))
    spots = []
    for shift in (0, 1):
        where = [jax.random.randint(jax.random.fold_in(key, axis), (), 0, length) for axis, length in enumerate(result.shape)]
        where[longest] = (where[longest] + shift) % result.shape[longest]
        spots.append(tuple(where))
    return result.at[spots[0]].set(least).at[spots[1]].set(high)


def steps_of(key, dims, shards, least, largest):
    loudness = 1.0
    for dim, shards_of in shards:
        heights = jax.random.uniform(jax.random.fold_in(jax.random.fold_in(key, 6), dim), (shards_of,), jnp.float32, least / len(shards), largest / len(shards))
        loudness = loudness * jnp.repeat(jnp.exp(heights), dims[dim] // shards_of).reshape((-1,) + (1,) * (len(dims) - 1 - dim))
    return loudness


def gaussian(stream_key, shape, width, limit, split=(), kind=jnp.bfloat16):
    entries = jax.random.normal(stream_key, shape, jnp.float32) * width
    if len(split) > 0:
        entries = steps_of(stream_key, shape, split, -0.22, 0.18) * entries
    return jnp.clip(entries, min=-limit, max=limit).astype(kind)


def setup_inputs(seed: int = 0) -> dict:
    streams_of = jax.random.split(jax.random.key(seed), 8)
    return {
        "density": draw_density(jax.random.fold_in(streams_of[7], 71), 0),
        "susceptibility": draw_susceptibility(jax.random.fold_in(streams_of[7], 71), 0),
        "station_cell": with_ends(jax.random.randint(streams_of[2], (2, STATIONS), 0, NX * NY), jax.random.fold_in(streams_of[2], 1), 0, (NX * NY) - 1).astype(jnp.int32),
        "station_line": draw_station_line(jax.random.fold_in(streams_of[7], 71), 0),
        "observed": gaussian(streams_of[4], (2, STATIONS), 0.5, 3.0, ((1, 4),), jnp.float32),
        "data_weight": jnp.clip(jnp.exp(math.log(2.0) - 1.3862944 * jax.random.uniform(streams_of[5], (2, STATIONS), jnp.float32) ** steps_of(streams_of[5], (2, STATIONS), ((1, 4),), -0.2, 0.2)), 0.5, 2.0),
        "trial_steps": jnp.clip(jnp.exp(jax.random.uniform(streams_of[6], (TRIALS,), jnp.float32, math.log(0.05), math.log(0.5))), 0.05, 0.5),
    }


cell_depth = 2.0
lift = 1.0
coupling_scale = 0.05
highest = lax.Precision.HIGHEST

def kernel_tile(field, station_x, station_y, cell_x, cell_y, depth):
    gap_x = station_x[:, None] - cell_x[None, :]
    gap_y = station_y[:, None] - cell_y[None, :]
    depth_row = depth[None, :]
    radius_sq = gap_x * gap_x + gap_y * gap_y + depth_row * depth_row
    inverse = lax.rsqrt(radius_sq)
    cube = inverse * inverse * inverse
    if field == 0:
        return depth_row * cube
    return (3.0 * depth_row * depth_row - radius_sq) * cube * inverse * inverse

def cell_coords(start, count):
    position = start + jnp.arange(count, dtype=jnp.int32)
    cell_x = (position // (NY * NZ)).astype(jnp.float32)
    cell_y = (position // NZ % NY).astype(jnp.float32)
    depth = ((position % NZ).astype(jnp.float32) + 0.5) * cell_depth + lift
    return (cell_x, cell_y, depth)

def forward_all(models, station_x, station_y):
    flat = models.reshape(2, -1)
    cells = flat.shape[1]
    block = math.gcd(cells, 8192)

    def turn(index, total):
        start = (index * block).astype(jnp.int32)
        cell_x, cell_y, depth = cell_coords(start, block)
        piece = lax.dynamic_slice_in_dim(flat, start, block, 1)
        rows = [jnp.dot(kernel_tile(field, station_x[field], station_y[field], cell_x, cell_y, depth), piece[field], precision=highest) for field in range(2)]
        return total + jnp.stack(rows)
    return lax.fori_loop(0, cells // block, turn, jnp.zeros((2, station_x.shape[1]), jnp.float32))

def adjoint_all(source, station_x, station_y):
    cells = NX * NY * NZ
    block = math.gcd(cells, 8192)

    def turn(index):
        start = (index * block).astype(jnp.int32)
        cell_x, cell_y, depth = cell_coords(start, block)
        rows = [jnp.dot(source[field], kernel_tile(field, station_x[field], station_y[field], cell_x, cell_y, depth), precision=highest) for field in range(2)]
        return jnp.stack(rows)
    parts = lax.map(turn, jnp.arange(cells // block, dtype=jnp.int32))
    return jnp.swapaxes(parts, 0, 1).reshape(2, NX, NY, NZ)

def forward_diffs(field):
    along_x = jnp.concatenate([field[1:] - field[:-1], jnp.zeros_like(field[:1])], axis=0)
    along_y = jnp.concatenate([field[:, 1:] - field[:, :-1], jnp.zeros_like(field[:, :1])], axis=1)
    along_z = jnp.concatenate([field[:, :, 1:] - field[:, :, :-1], jnp.zeros_like(field[:, :, :1])], axis=2)
    return (along_x, along_y, along_z)

def cross_energy(models):
    first_x, first_y, first_z = forward_diffs(models[0])
    second_x, second_y, second_z = forward_diffs(models[1])
    part_one = first_y * second_z - first_z * second_y
    part_two = first_z * second_x - first_x * second_z
    part_three = first_x * second_y - first_y * second_x
    return 0.5 * jnp.sum(part_one * part_one + part_two * part_two + part_three * part_three)

def level(values, lines):

    def one(value_row, line_row):
        sums = jax.ops.segment_sum(value_row, line_row, LINES)
        counts = jax.ops.segment_sum(jnp.ones_like(value_row), line_row, LINES)
        means = sums / jnp.maximum(counts, 1.0)
        return value_row - means[line_row]
    return jax.vmap(one)(values, lines)

def reference(density, susceptibility, station_cell, station_line, observed, data_weight, trial_steps):
    models = jnp.stack([density, susceptibility])
    station_x = (station_cell // NY).astype(jnp.float32)
    station_y = (station_cell % NY).astype(jnp.float32)
    total_stations = station_cell.shape[1]
    predicted = forward_all(models, station_x, station_y)
    residual = level(predicted - observed, station_line)
    weighted_residual = data_weight * residual
    source = level(data_weight * weighted_residual, station_line)
    data_gradient = adjoint_all(source, station_x, station_y)
    cross_force = jax.grad(cross_energy)(models)
    coupling = coupling_scale * total_stations / (NX * NY * NZ)
    gradient = data_gradient + coupling * cross_force
    peak = jnp.max(jnp.abs(gradient)) + 1e-06
    direction = gradient / peak
    image = forward_all(direction, station_x, station_y)
    change = level(image, station_line)
    values = []
    for trial in range(TRIALS):
        step = trial_steps[trial]
        moved = data_weight * (residual - step * change)
        values.append((0.5 * jnp.sum(moved * moved) + coupling * cross_energy(models - step * direction)) / (2 * total_stations))
    return (data_gradient, cross_force, weighted_residual, jnp.stack(values))
```

```python
import jax
import jax.numpy as jnp
from jax import lax
from jax.sharding import PartitionSpec as P

LINES = 256

cell_depth = 2.0
lift = 1.0
coupling_scale = 0.05
highest = lax.Precision.HIGHEST


def extended(block, low, high):
    for axis, dim in (("gx", 1), ("gy", 2)):
        count = lax.axis_size(axis)
        forward = [(i, i + 1) for i in range(count - 1)]
        backward = [(target, source) for source, target in forward]
        size = block.shape[dim]
        before = lax.ppermute(
            lax.slice_in_dim(block, size - low, None, axis=dim), axis, forward
        )
        after = lax.ppermute(lax.slice_in_dim(block, 0, high, axis=dim), axis, backward)
        block = jnp.concatenate([before, block, after], axis=dim)
    return block


def tables(first_x, first_y, rows, width, layers):
    shape = (rows, width, layers)
    gap_x = (first_x + lax.broadcasted_iota(jnp.int32, shape, 0)).astype(jnp.float32)
    gap_y = (first_y + lax.broadcasted_iota(jnp.int32, shape, 1)).astype(jnp.float32)
    depth = (
        lax.broadcasted_iota(jnp.int32, shape, 2).astype(jnp.float32) + 0.5
    ) * cell_depth + lift
    radius_sq = gap_x * gap_x + gap_y * gap_y + depth * depth
    inverse = lax.rsqrt(radius_sq)
    cube = inverse * inverse * inverse
    gravity = depth * cube
    magnetic = (3.0 * depth * depth - radius_sq) * cube * inverse * inverse
    return jnp.stack([gravity, magnetic])


def masks(rows, width, start_x, start_y, total_x, total_y):
    global_x = start_x + jnp.arange(rows, dtype=jnp.int32)
    global_y = start_y + jnp.arange(width, dtype=jnp.int32)
    mask_x = ((global_x >= 0) & (global_x < total_x - 1)).astype(jnp.float32)[:, None, None]
    mask_y = ((global_y >= 0) & (global_y < total_y - 1)).astype(jnp.float32)[None, :, None]
    valid = (global_x >= 0)[:, None] & (global_y >= 0)[None, :]
    valid = valid & (global_x < total_x)[:, None] & (global_y < total_y)[None, :]
    return (mask_x, mask_y, valid.astype(jnp.float32)[:, :, None])


def differences(field, mask_x, mask_y):
    base = field[:-1, :-1, :]
    along_x = (field[1:, :-1, :] - base) * mask_x
    along_y = (field[:-1, 1:, :] - base) * mask_y
    along_z = jnp.concatenate(
        [base[:, :, 1:] - base[:, :, :-1], jnp.zeros_like(base[:, :, :1])], axis=2
    )
    return (along_x, along_y, along_z)


def cross(a, b):
    return (
        a[1] * b[2] - a[2] * b[1],
        a[2] * b[0] - a[0] * b[2],
        a[0] * b[1] - a[1] * b[0],
    )


def inner(a, b):
    return a[0] * b[0] + a[1] * b[1] + a[2] * b[2]


def adjoint_differences(force, mask_x, mask_y):
    fx = force[0] * mask_x
    fy = force[1] * mask_y
    fz = force[2]
    keep = lax.broadcasted_iota(jnp.int32, fz.shape, 2) < fz.shape[2] - 1
    fz = jnp.where(keep, fz, 0.0)
    lower = jnp.concatenate([jnp.zeros_like(fz[:, :, :1]), fz[:, :, :-1]], axis=2)
    return (
        (fx[:-1, 1:] - fx[1:, 1:]) + (fy[1:, :-1] - fy[1:, 1:]) + (lower - fz)[1:, 1:]
    )


def from_all(values):
    count = lax.axis_size("gx") * lax.axis_size("gy")
    copies = jnp.broadcast_to(values[None], (count,) + values.shape)
    return lax.all_to_all(copies, ("gx", "gy"), 0, 0, tiled=True)


def everywhere(values):
    return jnp.sum(from_all(values), axis=0)


def all_groups(values):
    groups = lax.axis_size("gx")
    group = lax.axis_index("gx")
    pieces = jnp.stack(
        [values]
        + [
            lax.ppermute(values, "gx", [(i, (i + hop) % groups) for i in range(groups)])
            for hop in range(1, groups)
        ]
    )
    return jnp.concatenate(
        [
            lax.dynamic_index_in_dim(pieces, (group - turn) % groups, 0, keepdims=False)
            for turn in range(groups)
        ],
        axis=1,
    )


def body(density, susceptibility, station_cell, station_line, observed, data_weight, trial_steps):
    rows, width, layers = density.shape
    groups = lax.axis_size("gx")
    columns = lax.axis_size("gy")
    total_x = rows * groups
    total_y = width * columns
    stations = station_cell.shape[1] * groups
    group = lax.axis_index("gx")
    anchor_x = group * rows
    anchor_y = lax.axis_index("gy") * width
    coupling = coupling_scale * stations / (total_x * total_y * layers)
    models = jnp.stack([density, susceptibility])

    packed = jnp.concatenate(
        [
            station_cell.astype(jnp.float32),
            station_line.astype(jnp.float32),
            observed,
            data_weight,
        ]
    )
    packed = all_groups(packed)
    cells = packed[0:2].astype(jnp.int32)
    lines = packed[2:4].astype(jnp.int32)
    observed = packed[4:6]
    weight = packed[6:8]
    hot_x = (cells // total_y)[:, :, None] == jnp.arange(total_x, dtype=jnp.int32)
    hot_y = (cells % total_y)[:, :, None] == jnp.arange(total_y, dtype=jnp.int32)
    hot_x = hot_x.astype(jnp.float32)
    hot_y = hot_y.astype(jnp.float32)
    same = (lines[:, :, None] == lines[:, None, :]).astype(jnp.bfloat16)
    counts = jnp.sum(same.astype(jnp.float32), axis=2)

    def parts_of(values):
        first = lax.reduce_precision(values, 8, 7)
        rest = values - first
        second = lax.reduce_precision(rest, 8, 7)
        return jnp.stack([first, second, rest - second], axis=1).astype(jnp.bfloat16)

    def level(values):
        sums = jnp.einsum(
            "fct,fts->fcs", parts_of(values), same, preferred_element_type=jnp.float32
        )
        return values - jnp.sum(sums, axis=1) / jnp.maximum(counts, 1.0)

    def at_stations(surface):
        picked = jnp.einsum("fsy,fxy->fsx", hot_y, surface, precision=highest)
        return jnp.sum(picked * hot_x, axis=2)

    span_x = total_x + rows
    span_y = -(-(total_y + width) // 8) * 8
    table = tables(-rows - anchor_x, -width - anchor_y, span_x, span_y, layers)
    flat = table.reshape(2, span_x * span_y, layers)

    def forward(fields):
        by_offset = jnp.einsum(
            "fck,fpk->fcp", fields.reshape(2, rows * width, layers), flat, precision=highest
        ).reshape(2, rows, width, span_x, span_y)
        over_x = sum(
            lax.slice_in_dim(by_offset[:, i], rows - i, rows - i + total_x, axis=2)
            for i in range(rows)
        )
        return sum(
            lax.slice_in_dim(over_x[:, j], width - j, width - j + total_y, axis=2)
            for j in range(width)
        )

    def adjoint(surface):
        padded = jnp.pad(
            surface, ((0, 0), (rows, rows), (width, span_y - total_y))
        )
        shifted = jnp.stack(
            [
                padded[:, i : i + span_x, j : j + span_y]
                for i in range(rows + 1)
                for j in range(width + 1)
            ],
            axis=1,
        )
        return jnp.einsum(
            "fcp,fpk->fck",
            shifted.reshape(2, (rows + 1) * (width + 1), span_x * span_y),
            flat,
            precision=highest,
        ).reshape(2, rows + 1, width + 1, layers)

    wide = extended(models, 1, 2)
    mask_x, mask_y, valid = masks(
        rows + 2, width + 2, anchor_x - 1, anchor_y - 1, total_x, total_y
    )
    a = differences(wide[0], mask_x, mask_y)
    b = differences(wide[1], mask_x, mask_y)
    t = tuple(part * valid for part in cross(a, b))
    pull_a = cross(b, t)
    pull_b = cross(t, a)
    force = jnp.stack(
        [
            adjoint_differences(pull_a, mask_x, mask_y),
            adjoint_differences(pull_b, mask_x, mask_y),
        ]
    )
    cross_force = force[:, :rows, :width]

    surface_shape = (2, total_x, total_y)
    predicted = everywhere(forward(models).reshape(-1, 128)).reshape(surface_shape)
    predicted = at_stations(predicted)
    residual = level(predicted - observed)
    weighted = weight * residual
    source = level(weight * weighted)
    surface = jnp.einsum("fsx,fsy->fxy", hot_x * source[:, :, None], hot_y, precision=highest)
    data_wide = adjoint(surface)
    data_gradient = data_wide[:, :rows, :width]
    gradient_wide = data_wide + coupling * force
    gradient = gradient_wide[:, :rows, :width]

    image_part = forward(gradient)
    own_a = tuple(part[1:-1, 1:-1] for part in a)
    own_b = tuple(part[1:-1, 1:-1] for part in b)
    own_t = tuple(part[1:-1, 1:-1] for part in t)
    own_mask = (mask_x[1:-1], mask_y[:, 1:-1])
    da = differences(gradient_wide[0], *own_mask)
    db = differences(gradient_wide[1], *own_mask)
    t1 = tuple(-(p + q) for p, q in zip(cross(da, own_b), cross(own_a, db)))
    t2 = cross(da, db)
    powers = jnp.stack(
        [
            jnp.sum(inner(own_t, own_t)),
            2.0 * jnp.sum(inner(own_t, t1)),
            jnp.sum(inner(t1, t1) + 2.0 * inner(own_t, t2)),
            2.0 * jnp.sum(inner(t1, t2)),
            jnp.sum(inner(t2, t2)),
        ]
    )
    surface_size = 2 * total_x * total_y
    tail = jnp.concatenate([powers, jnp.max(jnp.abs(gradient))[None]])
    sent = jnp.concatenate([image_part.reshape(surface_size), tail])
    sent = jnp.pad(sent, (0, -sent.shape[0] % 1024)).reshape(-1, 128)
    got = from_all(sent)
    total = jnp.sum(got, axis=0).reshape(-1)
    peak_row, peak_lane = divmod(surface_size + 5, 128)
    peak = jnp.max(got[:, peak_row, peak_lane]) + 1e-06
    image = at_stations(total[:surface_size].reshape(surface_shape)) / peak
    change = level(image)
    moved = weight * (residual - trial_steps[:, None, None] * change)
    data_value = 0.5 * jnp.sum(moved * moved, axis=(1, 2))
    sums = total[surface_size : surface_size + 5]
    ratio = trial_steps / peak
    energy = sums[4]
    for order in (3, 2, 1, 0):
        energy = energy * ratio + sums[order]
    trial_values = (data_value + coupling * 0.5 * energy) / (2 * stations)
    weighted_residual = lax.dynamic_slice_in_dim(
        weighted, group * station_cell.shape[1], station_cell.shape[1], 1
    )
    return (data_gradient, cross_force, weighted_residual, trial_values)


def solution(mesh):
    placed = (
        P("gx", "gy", None),
        P("gx", "gy", None),
        P(None, "gx"),
        P(None, "gx"),
        P(None, "gx"),
        P(None, "gx"),
        P(),
    )
    return jax.shard_map(
        body,
        mesh=mesh,
        in_specs=placed,
        out_specs=(P(None, "gx", "gy", None), P(None, "gx", "gy", None), P(None, "gx"), P()),
        check_vma=False,
    )
```

```python
import functools

import jax
import jax.numpy as jnp
from jax import lax
from jax.experimental import pallas as pl
from jax.experimental.pallas import tpu as pltpu
from jax.sharding import PartitionSpec as P

LINES = 256

cell_depth = 2.0
lift = 1.0
coupling_scale = 0.05
highest = lax.Precision.HIGHEST


def extended(block, low, high):
    for axis, dim in (("gx", 1), ("gy", 2)):
        count = lax.axis_size(axis)
        forward = [(i, i + 1) for i in range(count - 1)]
        backward = [(target, source) for source, target in forward]
        size = block.shape[dim]
        before = lax.ppermute(
            lax.slice_in_dim(block, size - low, None, axis=dim), axis, forward
        )
        after = lax.ppermute(lax.slice_in_dim(block, 0, high, axis=dim), axis, backward)
        block = jnp.concatenate([before, block, after], axis=dim)
    return block


def block_tables(first_x, first_y, span_y, start, count, layers):
    position = start + lax.broadcasted_iota(jnp.int32, (count, layers), 0)
    gap_x = first_x + (position // span_y).astype(jnp.float32)
    gap_y = first_y + (position % span_y).astype(jnp.float32)
    depth = (
        lax.broadcasted_iota(jnp.int32, (count, layers), 1).astype(jnp.float32) + 0.5
    ) * cell_depth + lift
    radius_sq = gap_x * gap_x + gap_y * gap_y + depth * depth
    inverse = lax.rsqrt(radius_sq)
    cube = inverse * inverse * inverse
    gravity = depth * cube
    magnetic = (3.0 * depth * depth - radius_sq) * cube * inverse * inverse
    return (gravity, magnetic)


def spread_rows(by_offset, out_ref, field, rows, width, span_y):
    length = by_offset.shape[1]
    over_y = None
    for j in range(width):
        piece = by_offset[j * rows : (j + 1) * rows]
        piece = pltpu.roll(piece, (length - (width - j)) % length, 1)
        over_y = piece if over_y is None else over_y + piece
    total = None
    for i in range(rows):
        piece = pltpu.roll(over_y[i : i + 1], (length - (rows - i) * span_y) % length, 1)
        total = piece if total is None else total + piece
    chunks = out_ref.shape[0] // 2
    for chunk in range(chunks):
        row = field * chunks + chunk
        out_ref[row : row + 1, :] = total[:, chunk * 128 : (chunk + 1) * 128]


def project(columns, table):
    return lax.dot_general(
        columns, table, (((1,), (1,)), ((), ())),
        precision=highest, preferred_element_type=jnp.float32,
    )


def first_kernel(sizes, first_ref, model_ref, table_ref, out_ref):
    rows, width, span_y = sizes
    length, layers = table_ref.shape[1:]
    first_x = first_ref[0].astype(jnp.float32)
    first_y = first_ref[1].astype(jnp.float32)
    step = 128

    def turn(index, carry):
        start = pl.multiple_of(index * step, step)
        pair = block_tables(first_x, first_y, span_y, start, step, layers)
        table_ref[0, pl.ds(start, step), :] = pair[0]
        table_ref[1, pl.ds(start, step), :] = pair[1]
        return carry

    lax.fori_loop(0, length // step, turn, 0)
    for field in range(2):
        spread_rows(
            project(model_ref[field], table_ref[field]), out_ref, field, rows, width, span_y
        )


def middle_kernel(sizes, surface_ref, table_ref, force_ref, data_ref, out_ref, shift_ref, grad_ref):
    rows, width, span_y = sizes
    length, layers = table_ref.shape[1:]
    chunks = surface_ref.shape[0] // 2
    tall = -(-(rows + 1) // 8) * 8
    shift_ref[...] = jnp.zeros_like(shift_ref)
    for field in range(2):
        pieces = [
            surface_ref[field * chunks + chunk : field * chunks + chunk + 1, :]
            for chunk in range(chunks)
        ]
        pieces.append(jnp.zeros((1, length - chunks * 128), jnp.float32))
        flat = jnp.concatenate(pieces, axis=1)
        for i in range(rows + 1):
            amount = (rows - i) * span_y
            shift_ref[i : i + 1, :] = pltpu.roll(flat, amount, 1) if amount else flat
        base = shift_ref[0:tall, :]
        for j in range(width):
            shift_ref[j * tall : (j + 1) * tall, :] = pltpu.roll(base, width - j, 1)
        shift_ref[width * tall : (width + 1) * tall, :] = base
        wide = jnp.dot(
            shift_ref[...], table_ref[field],
            precision=highest, preferred_element_type=jnp.float32,
        )
        for j in range(width + 1):
            for i in range(rows + 1):
                data_ref[field, i, j : j + 1, :] = wide[j * tall + i : j * tall + i + 1]
            if j < width:
                grad_ref[j * rows : (j + 1) * rows, :] = (
                    wide[j * tall : j * tall + rows] + force_ref[field, j]
                )
        spread_rows(
            project(grad_ref[...], table_ref[field]), out_ref, field, rows, width, span_y
        )


def masks(rows, width, start_x, start_y, total_x, total_y):
    global_x = start_x + jnp.arange(rows, dtype=jnp.int32)
    global_y = start_y + jnp.arange(width, dtype=jnp.int32)
    mask_x = ((global_x >= 0) & (global_x < total_x - 1)).astype(jnp.float32)[:, None, None]
    mask_y = ((global_y >= 0) & (global_y < total_y - 1)).astype(jnp.float32)[None, :, None]
    valid = (global_x >= 0)[:, None] & (global_y >= 0)[None, :]
    valid = valid & (global_x < total_x)[:, None] & (global_y < total_y)[None, :]
    return (mask_x, mask_y, valid.astype(jnp.float32)[:, :, None])


def differences(field, mask_x, mask_y):
    base = field[:-1, :-1, :]
    along_x = (field[1:, :-1, :] - base) * mask_x
    along_y = (field[:-1, 1:, :] - base) * mask_y
    along_z = jnp.concatenate(
        [base[:, :, 1:] - base[:, :, :-1], jnp.zeros_like(base[:, :, :1])], axis=2
    )
    return (along_x, along_y, along_z)


def cross(a, b):
    return (
        a[1] * b[2] - a[2] * b[1],
        a[2] * b[0] - a[0] * b[2],
        a[0] * b[1] - a[1] * b[0],
    )


def inner(a, b):
    return a[0] * b[0] + a[1] * b[1] + a[2] * b[2]


def adjoint_differences(force, mask_x, mask_y):
    fx = force[0] * mask_x
    fy = force[1] * mask_y
    fz = force[2]
    keep = lax.broadcasted_iota(jnp.int32, fz.shape, 2) < fz.shape[2] - 1
    fz = jnp.where(keep, fz, 0.0)
    lower = jnp.concatenate([jnp.zeros_like(fz[:, :, :1]), fz[:, :, :-1]], axis=2)
    return (
        (fx[:-1, 1:] - fx[1:, 1:]) + (fy[1:, :-1] - fy[1:, 1:]) + (lower - fz)[1:, 1:]
    )


def from_all(values):
    count = lax.axis_size("gx") * lax.axis_size("gy")
    copies = jnp.broadcast_to(values[None], (count,) + values.shape)
    return lax.all_to_all(copies, ("gx", "gy"), 0, 0, tiled=True)


def everywhere(values):
    return jnp.sum(from_all(values), axis=0)


def all_groups(values):
    groups = lax.axis_size("gx")
    group = lax.axis_index("gx")
    pieces = jnp.stack(
        [values]
        + [
            lax.ppermute(values, "gx", [(i, (i + hop) % groups) for i in range(groups)])
            for hop in range(1, groups)
        ]
    )
    return jnp.concatenate(
        [
            lax.dynamic_index_in_dim(pieces, (group - turn) % groups, 0, keepdims=False)
            for turn in range(groups)
        ],
        axis=1,
    )


def body(density, susceptibility, station_cell, station_line, observed, data_weight, trial_steps):
    rows, width, layers = density.shape
    groups = lax.axis_size("gx")
    columns = lax.axis_size("gy")
    total_x = rows * groups
    total_y = width * columns
    stations = station_cell.shape[1] * groups
    group = lax.axis_index("gx")
    anchor_x = group * rows
    anchor_y = lax.axis_index("gy") * width
    coupling = coupling_scale * stations / (total_x * total_y * layers)
    models = jnp.stack([density, susceptibility])

    packed = jnp.concatenate(
        [
            station_cell.astype(jnp.float32),
            station_line.astype(jnp.float32),
            observed,
            data_weight,
        ]
    )
    packed = all_groups(packed)
    cells = packed[0:2].astype(jnp.int32)
    lines = packed[2:4].astype(jnp.int32)
    observed = packed[4:6]
    weight = packed[6:8]
    hot_x = (cells // total_y)[:, :, None] == jnp.arange(total_x, dtype=jnp.int32)
    span_y = -(-(total_y + width) // 8) * 8
    surface_shape = (2, total_x, span_y)
    hot_y = (cells % total_y)[:, :, None] == jnp.arange(span_y, dtype=jnp.int32)
    hot_x = hot_x.astype(jnp.float32)
    hot_y = hot_y.astype(jnp.float32)
    same = (lines[:, :, None] == lines[:, None, :]).astype(jnp.bfloat16)
    counts = jnp.sum(same.astype(jnp.float32), axis=2)

    def parts_of(values):
        first = lax.reduce_precision(values, 8, 7)
        rest = values - first
        second = lax.reduce_precision(rest, 8, 7)
        return jnp.stack([first, second, rest - second], axis=1).astype(jnp.bfloat16)

    def level(values):
        sums = jnp.einsum(
            "fct,fts->fcs", parts_of(values), same, preferred_element_type=jnp.float32
        )
        return values - jnp.sum(sums, axis=1) / jnp.maximum(counts, 1.0)

    def at_stations(surface):
        picked = jnp.einsum("fsy,fxy->fsx", hot_y, surface, precision=highest)
        return jnp.sum(picked * hot_x, axis=2)

    sizes = (rows, width, span_y)
    length = -(-(total_x + rows) // 16) * 16 * span_y
    chunks = -(-total_x * span_y // 128)
    vmem = pl.BlockSpec(memory_space=pltpu.VMEM)
    surface_out = jax.ShapeDtypeStruct((2 * chunks, 128), jnp.float32)
    table_out = jax.ShapeDtypeStruct((2, length, layers), jnp.float32)
    wide_shape = (2, rows + 1, width + 1, layers)
    tall = -(-(rows + 1) // 8) * 8
    by_column = jnp.swapaxes(models, 1, 2).reshape(2, width * rows, layers)
    table, predicted = pl.pallas_call(
        functools.partial(first_kernel, sizes),
        in_specs=[pl.BlockSpec(memory_space=pltpu.SMEM), vmem],
        out_specs=(vmem, vmem),
        out_shape=(table_out, surface_out),
    )(jnp.stack([-rows - anchor_x, -width - anchor_y]), by_column)

    def on_surface(sums):
        return sums.reshape(2, chunks * 128)[:, : total_x * span_y].reshape(surface_shape)

    wide = extended(models, 1, 2)
    mask_x, mask_y, valid = masks(
        rows + 2, width + 2, anchor_x - 1, anchor_y - 1, total_x, total_y
    )
    a = differences(wide[0], mask_x, mask_y)
    b = differences(wide[1], mask_x, mask_y)
    t = tuple(part * valid for part in cross(a, b))
    pull_a = cross(b, t)
    pull_b = cross(t, a)
    force = jnp.stack(
        [
            adjoint_differences(pull_a, mask_x, mask_y),
            adjoint_differences(pull_b, mask_x, mask_y),
        ]
    )
    cross_force = force[:, :rows, :width]
    pulled = coupling * jnp.swapaxes(cross_force, 1, 2)

    predicted = at_stations(on_surface(everywhere(predicted)))
    residual = level(predicted - observed)
    weighted = weight * residual
    source = level(weight * weighted)
    surface = jnp.einsum("fsx,fsy->fxy", hot_x * source[:, :, None], hot_y, precision=highest)
    surface = surface.reshape(2, total_x * span_y)
    surface = jnp.pad(surface, ((0, 0), (0, chunks * 128 - total_x * span_y)))
    data_wide, image_part = pl.pallas_call(
        functools.partial(middle_kernel, sizes),
        in_specs=[vmem, vmem, vmem],
        out_specs=(vmem, vmem),
        out_shape=(jax.ShapeDtypeStruct(wide_shape, jnp.float32), surface_out),
        scratch_shapes=[
            pltpu.VMEM(((width + 1) * tall, length), jnp.float32),
            pltpu.VMEM((width * rows, layers), jnp.float32),
        ],
    )(surface.reshape(2 * chunks, 128), table, pulled)
    data_gradient = data_wide[:, :rows, :width]
    gradient_wide = data_wide + coupling * force
    gradient = gradient_wide[:, :rows, :width]

    own_a = tuple(part[1:-1, 1:-1] for part in a)
    own_b = tuple(part[1:-1, 1:-1] for part in b)
    own_t = tuple(part[1:-1, 1:-1] for part in t)
    own_mask = (mask_x[1:-1], mask_y[:, 1:-1])
    da = differences(gradient_wide[0], *own_mask)
    db = differences(gradient_wide[1], *own_mask)
    t1 = tuple(-(p + q) for p, q in zip(cross(da, own_b), cross(own_a, db)))
    t2 = cross(da, db)
    powers = jnp.stack(
        [
            jnp.sum(inner(own_t, own_t)),
            2.0 * jnp.sum(inner(own_t, t1)),
            jnp.sum(inner(t1, t1) + 2.0 * inner(own_t, t2)),
            2.0 * jnp.sum(inner(t1, t2)),
            jnp.sum(inner(t2, t2)),
        ]
    )
    tail = jnp.concatenate([powers, jnp.max(jnp.abs(gradient))[None]])
    tail = jnp.broadcast_to(tail[:, None], (6, 128))
    got = from_all(jnp.concatenate([image_part, jnp.pad(tail, ((0, 2), (0, 0)))]))
    total = jnp.sum(got, axis=0)
    peak = jnp.max(got[:, 2 * chunks + 5, 0]) + 1e-06
    image = at_stations(on_surface(total[: 2 * chunks])) / peak
    change = level(image)
    moved = weighted.reshape(1, -1) - trial_steps[:, None] * (weight * change).reshape(1, -1)
    data_value = 0.5 * jnp.sum(moved * moved, axis=1)
    sums = total[2 * chunks : 2 * chunks + 5, 0]
    ratio = trial_steps / peak
    energy = sums[4]
    for order in (3, 2, 1, 0):
        energy = energy * ratio + sums[order]
    trial_values = (data_value + coupling * 0.5 * energy) / (2 * stations)
    weighted_residual = lax.dynamic_slice_in_dim(
        weighted, group * station_cell.shape[1], station_cell.shape[1], 1
    )
    return (data_gradient, cross_force, weighted_residual, trial_values)


def solution(mesh):
    placed = (
        P("gx", "gy", None),
        P("gx", "gy", None),
        P(None, "gx"),
        P(None, "gx"),
        P(None, "gx"),
        P(None, "gx"),
        P(),
    )
    return jax.shard_map(
        body,
        mesh=mesh,
        in_specs=placed,
        out_specs=(P(None, "gx", "gy", None), P(None, "gx", "gy", None), P(None, "gx"), P()),
        check_vma=False,
    )
```

```python
import functools

import jax
import jax.numpy as jnp
from jax import lax
from jax.experimental import pallas as pl
from jax.experimental.pallas import tpu as pltpu
from jax.sharding import PartitionSpec as P

LINES = 256

cell_depth = 2.0
lift = 1.0
coupling_scale = 0.05
highest = lax.Precision.HIGHEST


def extended(block, low, high):
    for axis, dim in (("gx", 1), ("gy", 2)):
        count = lax.axis_size(axis)
        forward = [(i, i + 1) for i in range(count - 1)]
        backward = [(target, source) for source, target in forward]
        size = block.shape[dim]
        before = lax.ppermute(
            lax.slice_in_dim(block, size - low, None, axis=dim), axis, forward
        )
        after = lax.ppermute(lax.slice_in_dim(block, 0, high, axis=dim), axis, backward)
        block = jnp.concatenate([before, block, after], axis=dim)
    return block


def block_tables(first_x, first_y, span_y, start, count, layers):
    position = start + lax.broadcasted_iota(jnp.int32, (count, layers), 0)
    gap_x = first_x + (position // span_y).astype(jnp.float32)
    gap_y = first_y + (position % span_y).astype(jnp.float32)
    depth = (
        lax.broadcasted_iota(jnp.int32, (count, layers), 1).astype(jnp.float32) + 0.5
    ) * cell_depth + lift
    radius_sq = gap_x * gap_x + gap_y * gap_y + depth * depth
    inverse = lax.rsqrt(radius_sq)
    cube = inverse * inverse * inverse
    gravity = depth * cube
    magnetic = (3.0 * depth * depth - radius_sq) * cube * inverse * inverse
    return (gravity, magnetic)


def spread_rows(by_offset, out_ref, field, rows, width, span_y):
    length = by_offset.shape[1]
    over_y = None
    for j in range(width):
        piece = by_offset[j * rows : (j + 1) * rows]
        piece = pltpu.roll(piece, (length - (width - j)) % length, 1)
        over_y = piece if over_y is None else over_y + piece
    total = None
    for i in range(rows):
        piece = pltpu.roll(over_y[i : i + 1], (length - (rows - i) * span_y) % length, 1)
        total = piece if total is None else total + piece
    chunks = out_ref.shape[0] // 2
    for chunk in range(chunks):
        row = field * chunks + chunk
        out_ref[row : row + 1, :] = total[:, chunk * 128 : (chunk + 1) * 128]


def project(columns, table):
    return lax.dot_general(
        columns, table, (((1,), (1,)), ((), ())),
        precision=highest, preferred_element_type=jnp.float32,
    )


def first_kernel(sizes, first_ref, model_ref, table_ref, out_ref):
    rows, width, span_y = sizes
    length, layers = table_ref.shape[1:]
    first_x = first_ref[0].astype(jnp.float32)
    first_y = first_ref[1].astype(jnp.float32)
    step = 128

    def turn(index, carry):
        start = pl.multiple_of(index * step, step)
        pair = block_tables(first_x, first_y, span_y, start, step, layers)
        table_ref[0, pl.ds(start, step), :] = pair[0]
        table_ref[1, pl.ds(start, step), :] = pair[1]
        return carry

    lax.fori_loop(0, length // step, turn, 0)
    for field in range(2):
        spread_rows(
            project(model_ref[field], table_ref[field]), out_ref, field, rows, width, span_y
        )


def middle_kernel(sizes, surface_ref, table_ref, force_ref, data_ref, out_ref, shift_ref, grad_ref):
    rows, width, span_y = sizes
    length, layers = table_ref.shape[1:]
    chunks = surface_ref.shape[0] // 2
    tall = -(-(rows + 1) // 8) * 8
    shift_ref[...] = jnp.zeros_like(shift_ref)
    for field in range(2):
        pieces = [
            surface_ref[field * chunks + chunk : field * chunks + chunk + 1, :]
            for chunk in range(chunks)
        ]
        pieces.append(jnp.zeros((1, length - chunks * 128), jnp.float32))
        flat = jnp.concatenate(pieces, axis=1)
        for i in range(rows + 1):
            amount = (rows - i) * span_y
            shift_ref[i : i + 1, :] = pltpu.roll(flat, amount, 1) if amount else flat
        base = shift_ref[0:tall, :]
        for j in range(width):
            shift_ref[j * tall : (j + 1) * tall, :] = pltpu.roll(base, width - j, 1)
        shift_ref[width * tall : (width + 1) * tall, :] = base
        wide = jnp.dot(
            shift_ref[...], table_ref[field],
            precision=highest, preferred_element_type=jnp.float32,
        )
        for j in range(width + 1):
            for i in range(rows + 1):
                data_ref[field, i, j : j + 1, :] = wide[j * tall + i : j * tall + i + 1]
            if j < width:
                grad_ref[j * rows : (j + 1) * rows, :] = (
                    wide[j * tall : j * tall + rows] + force_ref[field, j]
                )
        spread_rows(
            project(grad_ref[...], table_ref[field]), out_ref, field, rows, width, span_y
        )


def parts_of(values):
    first = values.astype(jnp.bfloat16)
    rest = values - first.astype(jnp.float32)
    second = rest.astype(jnp.bfloat16)
    third = (rest - second.astype(jnp.float32)).astype(jnp.bfloat16)
    return jnp.concatenate([first, second, third], axis=0)


def hot_rows(indices, size, kind=jnp.float32):
    labels = lax.broadcasted_iota(jnp.int32, (size, indices.shape[1]), 0)
    return (labels == indices).astype(jnp.float32).astype(kind)


def leveller(lines):
    hot = hot_rows(lines, LINES, jnp.bfloat16)
    over = (((1,), (1,)), ((), ()))
    ones = jnp.ones((8, lines.shape[1]), jnp.bfloat16)
    counts = lax.dot_general(ones, hot, over, preferred_element_type=jnp.float32)[0:1]
    counts = jnp.maximum(counts, 1.0)

    def level(values):
        sums = lax.dot_general(parts_of(values), hot, over, preferred_element_type=jnp.float32)
        means = jnp.sum(sums, axis=0, keepdims=True) / counts
        spread = jnp.dot(parts_of(means), hot, preferred_element_type=jnp.float32)
        return values - jnp.sum(spread, axis=0, keepdims=True)

    return level


def places(cells, total_y, surface):
    hot_x = hot_rows(cells // total_y, surface.shape[0])
    hot_y = hot_rows(cells % total_y, surface.shape[1])
    return hot_x, hot_y


def at_stations(surface, hot_x, hot_y):
    picked = jnp.dot(surface, hot_y, precision=highest, preferred_element_type=jnp.float32)
    return jnp.sum(picked * hot_x, axis=0, keepdims=True)


def source_kernel(total_y, surface_ref, packed_ref, weighted_ref, source_ref):
    for field in range(2):
        cells = packed_ref[field : field + 1, :].astype(jnp.int32)
        level = leveller(packed_ref[2 + field : 3 + field, :].astype(jnp.int32))
        weight = packed_ref[6 + field : 7 + field, :]
        hot_x, hot_y = places(cells, total_y, surface_ref[field])
        predicted = at_stations(surface_ref[field], hot_x, hot_y)
        weighted = weight * level(predicted - packed_ref[4 + field : 5 + field, :])
        weighted_ref[field : field + 1, :] = weighted
        source = level(weight * weighted)
        source_ref[field] = project(hot_x * source, hot_y)


def trial_kernel(total_y, coupling, image_ref, tail_ref, packed_ref, weighted_ref, step_ref, out_ref):
    peak = jnp.max(tail_ref[5:6, :], axis=1, keepdims=True) + 1e-06
    steps = step_ref[...]
    ratio = steps / peak
    energy = jnp.sum(tail_ref[4:5, :], axis=1, keepdims=True)
    for order in (3, 2, 1, 0):
        energy = energy * ratio + jnp.sum(tail_ref[order : order + 1, :], axis=1, keepdims=True)
    value = coupling * energy
    for field in range(2):
        cells = packed_ref[field : field + 1, :].astype(jnp.int32)
        level = leveller(packed_ref[2 + field : 3 + field, :].astype(jnp.int32))
        hot_x, hot_y = places(cells, total_y, image_ref[field])
        image = at_stations(image_ref[field], hot_x, hot_y) / peak
        change = packed_ref[6 + field : 7 + field, :] * level(image)
        moved = weighted_ref[field : field + 1, :] - steps * change
        value = value + jnp.sum(moved * moved, axis=1, keepdims=True)
    stations = 2 * packed_ref.shape[1]
    out_ref[...] = 0.5 * value / stations


def masks(rows, width, start_x, start_y, total_x, total_y):
    global_x = start_x + jnp.arange(rows, dtype=jnp.int32)
    global_y = start_y + jnp.arange(width, dtype=jnp.int32)
    mask_x = ((global_x >= 0) & (global_x < total_x - 1)).astype(jnp.float32)[:, None, None]
    mask_y = ((global_y >= 0) & (global_y < total_y - 1)).astype(jnp.float32)[None, :, None]
    valid = (global_x >= 0)[:, None] & (global_y >= 0)[None, :]
    valid = valid & (global_x < total_x)[:, None] & (global_y < total_y)[None, :]
    return (mask_x, mask_y, valid.astype(jnp.float32)[:, :, None])


def differences(field, mask_x, mask_y):
    base = field[:-1, :-1, :]
    along_x = (field[1:, :-1, :] - base) * mask_x
    along_y = (field[:-1, 1:, :] - base) * mask_y
    along_z = jnp.concatenate(
        [base[:, :, 1:] - base[:, :, :-1], jnp.zeros_like(base[:, :, :1])], axis=2
    )
    return (along_x, along_y, along_z)


def cross(a, b):
    return (
        a[1] * b[2] - a[2] * b[1],
        a[2] * b[0] - a[0] * b[2],
        a[0] * b[1] - a[1] * b[0],
    )


def inner(a, b):
    return a[0] * b[0] + a[1] * b[1] + a[2] * b[2]


def adjoint_differences(force, mask_x, mask_y):
    fx = force[0] * mask_x
    fy = force[1] * mask_y
    fz = force[2]
    keep = lax.broadcasted_iota(jnp.int32, fz.shape, 2) < fz.shape[2] - 1
    fz = jnp.where(keep, fz, 0.0)
    lower = jnp.concatenate([jnp.zeros_like(fz[:, :, :1]), fz[:, :, :-1]], axis=2)
    return (
        (fx[:-1, 1:] - fx[1:, 1:]) + (fy[1:, :-1] - fy[1:, 1:]) + (lower - fz)[1:, 1:]
    )


def from_all(values):
    count = lax.axis_size("gx") * lax.axis_size("gy")
    copies = jnp.broadcast_to(values[None], (count,) + values.shape)
    return lax.all_to_all(copies, ("gx", "gy"), 0, 0, tiled=True)


def everywhere(values):
    return jnp.sum(from_all(values), axis=0)


def doubled(values, largest):
    is_largest = lax.broadcasted_iota(jnp.int32, values.shape, 0) == largest
    for axis in ("gy", "gx"):
        count = lax.axis_size(axis)
        hop = 1
        while hop < count:
            other = lax.ppermute(values, axis, [(i, i ^ hop) for i in range(count)])
            values = jnp.where(is_largest, jnp.maximum(values, other), values + other)
            hop *= 2
    return values


def all_groups(values):
    groups = lax.axis_size("gx")
    group = lax.axis_index("gx")
    pieces = jnp.stack(
        [values]
        + [
            lax.ppermute(values, "gx", [(i, (i + hop) % groups) for i in range(groups)])
            for hop in range(1, groups)
        ]
    )
    return jnp.concatenate(
        [
            lax.dynamic_index_in_dim(pieces, (group - turn) % groups, 0, keepdims=False)
            for turn in range(groups)
        ],
        axis=1,
    )


def body(density, susceptibility, station_cell, station_line, observed, data_weight, trial_steps):
    rows, width, layers = density.shape
    groups = lax.axis_size("gx")
    columns = lax.axis_size("gy")
    total_x = rows * groups
    total_y = width * columns
    stations = station_cell.shape[1] * groups
    group = lax.axis_index("gx")
    anchor_x = group * rows
    anchor_y = lax.axis_index("gy") * width
    coupling = coupling_scale * stations / (total_x * total_y * layers)
    models = jnp.stack([density, susceptibility])

    packed = jnp.concatenate(
        [
            station_cell.astype(jnp.float32),
            station_line.astype(jnp.float32),
            observed,
            data_weight,
        ]
    )
    packed = all_groups(packed)
    span_y = -(-(total_y + width) // 8) * 8
    surface_shape = (2, total_x, span_y)
    sizes = (rows, width, span_y)
    length = -(-(total_x + rows) // 16) * 16 * span_y
    chunks = -(-total_x * span_y // 128)
    vmem = pl.BlockSpec(memory_space=pltpu.VMEM)
    surface_out = jax.ShapeDtypeStruct((2 * chunks, 128), jnp.float32)
    table_out = jax.ShapeDtypeStruct((2, length, layers), jnp.float32)
    wide_shape = (2, rows + 1, width + 1, layers)
    tall = -(-(rows + 1) // 8) * 8
    by_column = jnp.swapaxes(models, 1, 2).reshape(2, width * rows, layers)
    table, predicted = pl.pallas_call(
        functools.partial(first_kernel, sizes),
        in_specs=[pl.BlockSpec(memory_space=pltpu.SMEM), vmem],
        out_specs=(vmem, vmem),
        out_shape=(table_out, surface_out),
    )(jnp.stack([-rows - anchor_x, -width - anchor_y]), by_column)

    def on_surface(sums):
        return sums.reshape(2, chunks * 128)[:, : total_x * span_y].reshape(surface_shape)

    wide = extended(models, 1, 2)
    mask_x, mask_y, valid = masks(
        rows + 2, width + 2, anchor_x - 1, anchor_y - 1, total_x, total_y
    )
    a = differences(wide[0], mask_x, mask_y)
    b = differences(wide[1], mask_x, mask_y)
    t = tuple(part * valid for part in cross(a, b))
    pull_a = cross(b, t)
    pull_b = cross(t, a)
    force = jnp.stack(
        [
            adjoint_differences(pull_a, mask_x, mask_y),
            adjoint_differences(pull_b, mask_x, mask_y),
        ]
    )
    cross_force = force[:, :rows, :width]
    pulled = coupling * jnp.swapaxes(cross_force, 1, 2)

    weighted, surface = pl.pallas_call(
        functools.partial(source_kernel, total_y),
        in_specs=[vmem, vmem],
        out_specs=(vmem, vmem),
        out_shape=(
            jax.ShapeDtypeStruct((2, stations), jnp.float32),
            jax.ShapeDtypeStruct(surface_shape, jnp.float32),
        ),
    )(on_surface(everywhere(predicted)), packed)
    surface = surface.reshape(2, total_x * span_y)
    surface = jnp.pad(surface, ((0, 0), (0, chunks * 128 - total_x * span_y)))
    data_wide, image_part = pl.pallas_call(
        functools.partial(middle_kernel, sizes),
        in_specs=[vmem, vmem, vmem],
        out_specs=(vmem, vmem),
        out_shape=(jax.ShapeDtypeStruct(wide_shape, jnp.float32), surface_out),
        scratch_shapes=[
            pltpu.VMEM(((width + 1) * tall, length), jnp.float32),
            pltpu.VMEM((width * rows, layers), jnp.float32),
        ],
    )(surface.reshape(2 * chunks, 128), table, pulled)
    data_gradient = data_wide[:, :rows, :width]
    gradient_wide = data_wide + coupling * force
    gradient = gradient_wide[:, :rows, :width]

    own_a = tuple(part[1:-1, 1:-1] for part in a)
    own_b = tuple(part[1:-1, 1:-1] for part in b)
    own_t = tuple(part[1:-1, 1:-1] for part in t)
    own_mask = (mask_x[1:-1], mask_y[:, 1:-1])
    da = differences(gradient_wide[0], *own_mask)
    db = differences(gradient_wide[1], *own_mask)
    t1 = tuple(-(p + q) for p, q in zip(cross(da, own_b), cross(own_a, db)))
    t2 = cross(da, db)
    def lanes(values):
        return jnp.sum(values, axis=(0, 1))[None]

    tail = (
        lanes(inner(own_t, own_t)),
        lanes(2.0 * inner(own_t, t1)),
        lanes(inner(t1, t1) + 2.0 * inner(own_t, t2)),
        lanes(2.0 * inner(t1, t2)),
        lanes(inner(t2, t2)),
        jnp.max(jnp.abs(gradient), axis=(0, 1, 2))[None],
        jnp.zeros((2, layers), jnp.float32),
    )
    total = doubled(jnp.concatenate((image_part,) + tail), 2 * chunks + 5)
    trial_values = pl.pallas_call(
        functools.partial(trial_kernel, total_y, coupling),
        in_specs=[vmem] * 5,
        out_specs=vmem,
        out_shape=jax.ShapeDtypeStruct((trial_steps.shape[0], 1), jnp.float32),
    )(
        on_surface(total[: 2 * chunks]),
        total[2 * chunks :],
        packed,
        weighted,
        trial_steps[:, None],
    )[:, 0]
    weighted_residual = lax.dynamic_slice_in_dim(
        weighted, group * station_cell.shape[1], station_cell.shape[1], 1
    )
    return (data_gradient, cross_force, weighted_residual, trial_values)


def solution(mesh):
    placed = (
        P("gx", "gy", None),
        P("gx", "gy", None),
        P(None, "gx"),
        P(None, "gx"),
        P(None, "gx"),
        P(None, "gx"),
        P(),
    )
    return jax.shard_map(
        body,
        mesh=mesh,
        in_specs=placed,
        out_specs=(P(None, "gx", "gy", None), P(None, "gx", "gy", None), P(None, "gx"), P()),
        check_vma=False,
    )
```

```python
import functools

import jax
import jax.numpy as jnp
from jax import lax
from jax.experimental import pallas as pl
from jax.experimental.pallas import tpu as pltpu
from jax.sharding import PartitionSpec as P

LINES = 256

cell_depth = 2.0
lift = 1.0
coupling_scale = 0.05
highest = lax.Precision.HIGHEST


def extended(block, low, high):
    for axis, dim in (("gx", 1), ("gy", 2)):
        count = lax.axis_size(axis)
        forward = [(i, i + 1) for i in range(count - 1)]
        backward = [(target, source) for source, target in forward]
        size = block.shape[dim]
        before = lax.ppermute(
            lax.slice_in_dim(block, size - low, None, axis=dim), axis, forward
        )
        after = lax.ppermute(lax.slice_in_dim(block, 0, high, axis=dim), axis, backward)
        block = jnp.concatenate([before, block, after], axis=dim)
    return block


def block_tables(first_x, first_y, span_y, start, count, layers):
    position = start + lax.broadcasted_iota(jnp.int32, (count, layers), 0)
    gap_x = first_x + (position // span_y).astype(jnp.float32)
    gap_y = first_y + (position % span_y).astype(jnp.float32)
    depth = (
        lax.broadcasted_iota(jnp.int32, (count, layers), 1).astype(jnp.float32) + 0.5
    ) * cell_depth + lift
    radius_sq = gap_x * gap_x + gap_y * gap_y + depth * depth
    inverse = lax.rsqrt(radius_sq)
    cube = inverse * inverse * inverse
    gravity = depth * cube
    magnetic = (3.0 * depth * depth - radius_sq) * cube * inverse * inverse
    return (gravity, magnetic)


def spread_rows(by_offset, out_ref, field, rows, width, span_y):
    length = by_offset.shape[1]
    over_y = None
    for j in range(width):
        piece = by_offset[j * rows : (j + 1) * rows]
        piece = pltpu.roll(piece, (length - (width - j)) % length, 1)
        over_y = piece if over_y is None else over_y + piece
    total = None
    for i in range(rows):
        piece = pltpu.roll(over_y[i : i + 1], (length - (rows - i) * span_y) % length, 1)
        total = piece if total is None else total + piece
    chunks = out_ref.shape[0] // 2
    for chunk in range(chunks):
        row = field * chunks + chunk
        out_ref[row : row + 1, :] = total[:, chunk * 128 : (chunk + 1) * 128]


def project(columns, table):
    return lax.dot_general(
        columns, table, (((1,), (1,)), ((), ())),
        precision=highest, preferred_element_type=jnp.float32,
    )


def first_kernel(sizes, first_ref, model_ref, table_ref, out_ref):
    rows, width, span_y = sizes
    length, layers = table_ref.shape[1:]
    first_x = first_ref[0].astype(jnp.float32)
    first_y = first_ref[1].astype(jnp.float32)
    step = 128

    def turn(index, carry):
        start = pl.multiple_of(index * step, step)
        pair = block_tables(first_x, first_y, span_y, start, step, layers)
        table_ref[0, pl.ds(start, step), :] = pair[0]
        table_ref[1, pl.ds(start, step), :] = pair[1]
        return carry

    lax.fori_loop(0, length // step, turn, 0)
    for field in range(2):
        spread_rows(
            project(model_ref[field], table_ref[field]), out_ref, field, rows, width, span_y
        )


def middle_kernel(sizes, surface_ref, table_ref, force_ref, data_ref, out_ref, shift_ref, grad_ref):
    rows, width, span_y = sizes
    length, layers = table_ref.shape[1:]
    tall = -(-(rows + 1) // 8) * 8
    shift_ref[...] = jnp.zeros_like(shift_ref)
    for field in range(2):
        surface = surface_ref[field]
        pieces = [surface[row : row + 1, :] for row in range(surface.shape[0])]
        pieces.append(jnp.zeros((1, length - surface.size), jnp.float32))
        flat = jnp.concatenate(pieces, axis=1)
        for i in range(rows + 1):
            amount = (rows - i) * span_y
            shift_ref[i : i + 1, :] = pltpu.roll(flat, amount, 1) if amount else flat
        base = shift_ref[0:tall, :]
        for j in range(width):
            shift_ref[j * tall : (j + 1) * tall, :] = pltpu.roll(base, width - j, 1)
        shift_ref[width * tall : (width + 1) * tall, :] = base
        wide = jnp.dot(
            shift_ref[...], table_ref[field],
            precision=highest, preferred_element_type=jnp.float32,
        )
        for j in range(width + 1):
            for i in range(rows + 1):
                data_ref[field, i, j : j + 1, :] = wide[j * tall + i : j * tall + i + 1]
            if j < width:
                grad_ref[j * rows : (j + 1) * rows, :] = (
                    wide[j * tall : j * tall + rows] + force_ref[field, j]
                )
        spread_rows(
            project(grad_ref[...], table_ref[field]), out_ref, field, rows, width, span_y
        )


def parts_of(values):
    first = values.astype(jnp.bfloat16)
    rest = values - first.astype(jnp.float32)
    second = rest.astype(jnp.bfloat16)
    third = (rest - second.astype(jnp.float32)).astype(jnp.bfloat16)
    return jnp.concatenate([first, second, third], axis=0)


def hot_rows(indices, size, kind=jnp.float32):
    labels = lax.broadcasted_iota(jnp.int32, (size, indices.shape[1]), 0)
    return (labels == indices).astype(jnp.float32).astype(kind)


def leveller(lines):
    hot = hot_rows(lines, LINES, jnp.bfloat16)
    over = (((1,), (1,)), ((), ()))
    ones = jnp.ones((8, lines.shape[1]), jnp.bfloat16)
    counts = lax.dot_general(ones, hot, over, preferred_element_type=jnp.float32)[0:1]
    counts = jnp.maximum(counts, 1.0)

    def level(values):
        sums = lax.dot_general(parts_of(values), hot, over, preferred_element_type=jnp.float32)
        means = jnp.sum(sums, axis=0, keepdims=True) / counts
        spread = jnp.dot(parts_of(means), hot, preferred_element_type=jnp.float32)
        return values - jnp.sum(spread, axis=0, keepdims=True)

    return level


def places(cells, total_y, surface):
    hot_x = hot_rows(cells // total_y, surface.shape[0])
    hot_y = hot_rows(cells % total_y, surface.shape[1])
    return hot_x, hot_y


def at_stations(surface, hot_x, hot_y):
    count = surface.shape[0]
    parts = jnp.dot(
        parts_of(surface), hot_y.astype(jnp.bfloat16), preferred_element_type=jnp.float32
    )
    picked = parts[:count] + parts[count : 2 * count] + parts[2 * count :]
    return jnp.sum(picked * hot_x, axis=0, keepdims=True)


def to_surface(values, hot_x, hot_y):
    count = hot_x.shape[0]
    parts = lax.dot_general(
        parts_of(hot_x * values), hot_y.astype(jnp.bfloat16), (((1,), (1,)), ((), ())),
        preferred_element_type=jnp.float32,
    )
    return parts[:count] + parts[count : 2 * count] + parts[2 * count :]


def unpacked(flat_ref, field, chunks, surface_ref):
    pieces = [
        flat_ref[field * chunks + chunk : field * chunks + chunk + 1, :]
        for chunk in range(chunks)
    ]
    flat = jnp.concatenate(pieces, axis=1)
    rows, span_y = surface_ref.shape
    for row in range(rows):
        surface_ref[row : row + 1, :] = flat[:, row * span_y : (row + 1) * span_y]
    return surface_ref[...]


def source_kernel(total_y, surface_ref, packed_ref, weighted_ref, source_ref, hold_ref):
    for field in range(2):
        cells = packed_ref[field : field + 1, :].astype(jnp.int32)
        level = leveller(packed_ref[2 + field : 3 + field, :].astype(jnp.int32))
        weight = packed_ref[6 + field : 7 + field, :]
        surface = unpacked(surface_ref, field, surface_ref.shape[0] // 2, hold_ref)
        hot_x, hot_y = places(cells, total_y, surface)
        predicted = at_stations(surface, hot_x, hot_y)
        weighted = weight * level(predicted - packed_ref[4 + field : 5 + field, :])
        weighted_ref[field : field + 1, :] = weighted
        source = level(weight * weighted)
        source_ref[field] = to_surface(source, hot_x, hot_y)


def trial_kernel(total_y, coupling, total_ref, packed_ref, weighted_ref, step_ref, out_ref, hold_ref):
    chunks = total_ref.shape[0] // 2 - 4
    tail = total_ref[2 * chunks :, :]
    peak = jnp.max(tail[5:6, :], axis=1, keepdims=True) + 1e-06
    steps = step_ref[...]
    ratio = steps / peak
    energy = jnp.sum(tail[4:5, :], axis=1, keepdims=True)
    for order in (3, 2, 1, 0):
        energy = energy * ratio + jnp.sum(tail[order : order + 1, :], axis=1, keepdims=True)
    value = coupling * energy
    for field in range(2):
        cells = packed_ref[field : field + 1, :].astype(jnp.int32)
        level = leveller(packed_ref[2 + field : 3 + field, :].astype(jnp.int32))
        surface = unpacked(total_ref, field, chunks, hold_ref)
        hot_x, hot_y = places(cells, total_y, surface)
        image = at_stations(surface, hot_x, hot_y) / peak
        change = packed_ref[6 + field : 7 + field, :] * level(image)
        moved = weighted_ref[field : field + 1, :] - steps * change
        value = value + jnp.sum(moved * moved, axis=1, keepdims=True)
    stations = 2 * packed_ref.shape[1]
    count = value.shape[0]
    here = lax.broadcasted_iota(jnp.int32, (count, count), 0) == lax.broadcasted_iota(
        jnp.int32, (count, count), 1
    )
    out_ref[...] = jnp.sum(jnp.where(here, 0.5 * value / stations, 0.0), axis=0, keepdims=True)


def masks(rows, width, start_x, start_y, total_x, total_y):
    global_x = start_x + jnp.arange(rows, dtype=jnp.int32)
    global_y = start_y + jnp.arange(width, dtype=jnp.int32)
    mask_x = ((global_x >= 0) & (global_x < total_x - 1)).astype(jnp.float32)[:, None, None]
    mask_y = ((global_y >= 0) & (global_y < total_y - 1)).astype(jnp.float32)[None, :, None]
    valid = (global_x >= 0)[:, None] & (global_y >= 0)[None, :]
    valid = valid & (global_x < total_x)[:, None] & (global_y < total_y)[None, :]
    return (mask_x, mask_y, valid.astype(jnp.float32)[:, :, None])


def differences(field, mask_x, mask_y):
    base = field[:-1, :-1, :]
    along_x = (field[1:, :-1, :] - base) * mask_x
    along_y = (field[:-1, 1:, :] - base) * mask_y
    along_z = jnp.concatenate(
        [base[:, :, 1:] - base[:, :, :-1], jnp.zeros_like(base[:, :, :1])], axis=2
    )
    return (along_x, along_y, along_z)


def cross(a, b):
    return (
        a[1] * b[2] - a[2] * b[1],
        a[2] * b[0] - a[0] * b[2],
        a[0] * b[1] - a[1] * b[0],
    )


def inner(a, b):
    return a[0] * b[0] + a[1] * b[1] + a[2] * b[2]


def adjoint_differences(force, mask_x, mask_y):
    fx = force[0] * mask_x
    fy = force[1] * mask_y
    fz = force[2]
    keep = lax.broadcasted_iota(jnp.int32, fz.shape, 2) < fz.shape[2] - 1
    fz = jnp.where(keep, fz, 0.0)
    lower = jnp.concatenate([jnp.zeros_like(fz[:, :, :1]), fz[:, :, :-1]], axis=2)
    return (
        (fx[:-1, 1:] - fx[1:, 1:]) + (fy[1:, :-1] - fy[1:, 1:]) + (lower - fz)[1:, 1:]
    )


def from_all(values):
    count = lax.axis_size("gx") * lax.axis_size("gy")
    copies = jnp.broadcast_to(values[None], (count,) + values.shape)
    return lax.all_to_all(copies, ("gx", "gy"), 0, 0, tiled=True)


def everywhere(values):
    return jnp.sum(from_all(values), axis=0)


def doubled(values, largest):
    is_largest = lax.broadcasted_iota(jnp.int32, values.shape, 0) == largest
    for axis in ("gy", "gx"):
        count = lax.axis_size(axis)
        hop = 1
        while hop < count:
            other = lax.ppermute(values, axis, [(i, i ^ hop) for i in range(count)])
            values = jnp.where(is_largest, jnp.maximum(values, other), values + other)
            hop *= 2
    return values


def all_groups(values):
    groups = lax.axis_size("gx")
    group = lax.axis_index("gx")
    pieces = jnp.stack(
        [values]
        + [
            lax.ppermute(values, "gx", [(i, (i + hop) % groups) for i in range(groups)])
            for hop in range(1, groups)
        ]
    )
    return jnp.concatenate(
        [
            lax.dynamic_index_in_dim(pieces, (group - turn) % groups, 0, keepdims=False)
            for turn in range(groups)
        ],
        axis=1,
    )


def body(density, susceptibility, station_cell, station_line, observed, data_weight, trial_steps):
    rows, width, layers = density.shape
    groups = lax.axis_size("gx")
    columns = lax.axis_size("gy")
    total_x = rows * groups
    total_y = width * columns
    stations = station_cell.shape[1] * groups
    group = lax.axis_index("gx")
    anchor_x = group * rows
    anchor_y = lax.axis_index("gy") * width
    coupling = coupling_scale * stations / (total_x * total_y * layers)
    models = jnp.stack([density, susceptibility])

    packed = jnp.concatenate(
        [
            station_cell.astype(jnp.float32),
            station_line.astype(jnp.float32),
            observed,
            data_weight,
        ]
    )
    packed = all_groups(packed)
    span_y = -(-(total_y + width) // 8) * 8
    surface_shape = (2, total_x, span_y)
    sizes = (rows, width, span_y)
    length = -(-(total_x + rows) // 16) * 16 * span_y
    chunks = -(-total_x * span_y // 128)
    vmem = pl.BlockSpec(memory_space=pltpu.VMEM)
    surface_out = jax.ShapeDtypeStruct((2 * chunks, 128), jnp.float32)
    table_out = jax.ShapeDtypeStruct((2, length, layers), jnp.float32)
    wide_shape = (2, rows + 1, width + 1, layers)
    tall = -(-(rows + 1) // 8) * 8
    by_column = jnp.swapaxes(models, 1, 2).reshape(2, width * rows, layers)
    table, predicted = pl.pallas_call(
        functools.partial(first_kernel, sizes),
        in_specs=[pl.BlockSpec(memory_space=pltpu.SMEM), vmem],
        out_specs=(vmem, vmem),
        out_shape=(table_out, surface_out),
    )(jnp.stack([-rows - anchor_x, -width - anchor_y]), by_column)

    wide = extended(models, 1, 2)
    mask_x, mask_y, valid = masks(
        rows + 2, width + 2, anchor_x - 1, anchor_y - 1, total_x, total_y
    )
    a = differences(wide[0], mask_x, mask_y)
    b = differences(wide[1], mask_x, mask_y)
    t = tuple(part * valid for part in cross(a, b))
    pull_a = cross(b, t)
    pull_b = cross(t, a)
    force = jnp.stack(
        [
            adjoint_differences(pull_a, mask_x, mask_y),
            adjoint_differences(pull_b, mask_x, mask_y),
        ]
    )
    cross_force = force[:, :rows, :width]
    pulled = coupling * jnp.swapaxes(cross_force, 1, 2)

    weighted, surface = pl.pallas_call(
        functools.partial(source_kernel, total_y),
        in_specs=[vmem, vmem],
        out_specs=(vmem, vmem),
        out_shape=(
            jax.ShapeDtypeStruct((2, stations), jnp.float32),
            jax.ShapeDtypeStruct(surface_shape, jnp.float32),
        ),
        scratch_shapes=[pltpu.VMEM(surface_shape[1:], jnp.float32)],
    )(everywhere(predicted), packed)
    data_wide, image_part = pl.pallas_call(
        functools.partial(middle_kernel, sizes),
        in_specs=[vmem, vmem, vmem],
        out_specs=(vmem, vmem),
        out_shape=(jax.ShapeDtypeStruct(wide_shape, jnp.float32), surface_out),
        scratch_shapes=[
            pltpu.VMEM(((width + 1) * tall, length), jnp.float32),
            pltpu.VMEM((width * rows, layers), jnp.float32),
        ],
    )(surface, table, pulled)
    data_gradient = data_wide[:, :rows, :width]
    gradient_wide = data_wide + coupling * force
    gradient = gradient_wide[:, :rows, :width]

    own_a = tuple(part[1:-1, 1:-1] for part in a)
    own_b = tuple(part[1:-1, 1:-1] for part in b)
    own_t = tuple(part[1:-1, 1:-1] for part in t)
    own_mask = (mask_x[1:-1], mask_y[:, 1:-1])
    da = differences(gradient_wide[0], *own_mask)
    db = differences(gradient_wide[1], *own_mask)
    t1 = tuple(-(p + q) for p, q in zip(cross(da, own_b), cross(own_a, db)))
    t2 = cross(da, db)
    def lanes(values):
        return jnp.sum(values, axis=(0, 1))[None]

    tail = (
        lanes(inner(own_t, own_t)),
        lanes(2.0 * inner(own_t, t1)),
        lanes(inner(t1, t1) + 2.0 * inner(own_t, t2)),
        lanes(2.0 * inner(t1, t2)),
        lanes(inner(t2, t2)),
        jnp.max(jnp.abs(gradient), axis=(0, 1, 2))[None],
        jnp.zeros((2, layers), jnp.float32),
    )
    total = doubled(jnp.concatenate((image_part,) + tail), 2 * chunks + 5)
    trial_values = pl.pallas_call(
        functools.partial(trial_kernel, total_y, coupling),
        in_specs=[vmem] * 4,
        out_specs=vmem,
        out_shape=jax.ShapeDtypeStruct((1, trial_steps.shape[0]), jnp.float32),
        scratch_shapes=[pltpu.VMEM(surface_shape[1:], jnp.float32)],
    )(total, packed, weighted, trial_steps[:, None])
    trial_values = trial_values.reshape(-1)
    weighted_residual = lax.dynamic_slice_in_dim(
        weighted, group * station_cell.shape[1], station_cell.shape[1], 1
    )
    return (data_gradient, cross_force, weighted_residual, trial_values)


def solution(mesh):
    placed = (
        P("gx", "gy", None),
        P("gx", "gy", None),
        P(None, "gx"),
        P(None, "gx"),
        P(None, "gx"),
        P(None, "gx"),
        P(),
    )
    return jax.shard_map(
        body,
        mesh=mesh,
        in_specs=placed,
        out_specs=(P(None, "gx", "gy", None), P(None, "gx", "gy", None), P(None, "gx"), P()),
        check_vma=False,
    )
```

```python
import functools

import jax
import jax.numpy as jnp
from jax import lax
from jax.experimental import pallas as pl
from jax.experimental.pallas import tpu as pltpu
from jax.sharding import PartitionSpec as P

LINES = 256

cell_depth = 2.0
lift = 1.0
coupling_scale = 0.05


def extended(block, low, high):
    for axis, dim in (("gx", 1), ("gy", 2)):
        count = lax.axis_size(axis)
        forward = [(i, i + 1) for i in range(count - 1)]
        backward = [(target, source) for source, target in forward]
        size = block.shape[dim]
        before = lax.ppermute(
            lax.slice_in_dim(block, size - low, None, axis=dim), axis, forward
        )
        after = lax.ppermute(lax.slice_in_dim(block, 0, high, axis=dim), axis, backward)
        block = jnp.concatenate([before, block, after], axis=dim)
    return block


def block_tables(first_x, first_y, span_y, start, count, layers):
    position = start + lax.broadcasted_iota(jnp.int32, (count, layers), 0)
    gap_x = first_x + (position // span_y).astype(jnp.float32)
    gap_y = first_y + (position % span_y).astype(jnp.float32)
    depth = (
        lax.broadcasted_iota(jnp.int32, (count, layers), 1).astype(jnp.float32) + 0.5
    ) * cell_depth + lift
    radius_sq = gap_x * gap_x + gap_y * gap_y + depth * depth
    inverse = lax.rsqrt(radius_sq)
    cube = inverse * inverse * inverse
    gravity = depth * cube
    magnetic = (3.0 * depth * depth - radius_sq) * cube * inverse * inverse
    return (gravity, magnetic)


def spread_rows(by_offset, out_ref, field, rows, width, span_y):
    length = by_offset.shape[1]
    over_y = None
    for j in range(width):
        piece = by_offset[j * rows : (j + 1) * rows]
        piece = pltpu.roll(piece, (length - (width - j)) % length, 1)
        over_y = piece if over_y is None else over_y + piece
    total = None
    for i in range(rows):
        piece = pltpu.roll(over_y[i : i + 1], (length - (rows - i) * span_y) % length, 1)
        total = piece if total is None else total + piece
    chunks = out_ref.shape[0] // 2
    for chunk in range(chunks):
        row = field * chunks + chunk
        out_ref[row : row + 1, :] = total[:, chunk * 128 : (chunk + 1) * 128]


def two_parts(values):
    first = values.astype(jnp.bfloat16)
    return first, (values - first.astype(jnp.float32)).astype(jnp.bfloat16)


def product(left, right, side):
    high, low = two_parts(left)
    count = left.shape[0]
    right_high, right_low = two_parts(right)
    dims = (((1,), (side,)), ((), ()))
    both = lax.dot_general(
        jnp.concatenate([high, low], axis=0), right_high, dims,
        preferred_element_type=jnp.float32,
    )
    rest = lax.dot_general(high, right_low, dims, preferred_element_type=jnp.float32)
    return both[:count] + (both[count:] + rest)


def project(columns, table):
    return product(columns, table, 1)


def first_kernel(sizes, first_ref, model_ref, table_ref, out_ref):
    rows, width, span_y = sizes
    length, layers = table_ref.shape[1:]
    first_x = first_ref[0].astype(jnp.float32)
    first_y = first_ref[1].astype(jnp.float32)
    step = 128

    def turn(index, carry):
        start = pl.multiple_of(index * step, step)
        pair = block_tables(first_x, first_y, span_y, start, step, layers)
        table_ref[0, pl.ds(start, step), :] = pair[0]
        table_ref[1, pl.ds(start, step), :] = pair[1]
        return carry

    lax.fori_loop(0, length // step, turn, 0)
    for field in range(2):
        spread_rows(
            project(model_ref[field], table_ref[field]), out_ref, field, rows, width, span_y
        )


def middle_kernel(sizes, surface_ref, table_ref, force_ref, data_ref, out_ref, shift_ref, grad_ref):
    rows, width, span_y = sizes
    length, layers = table_ref.shape[1:]
    tall = -(-(rows + 1) // 8) * 8
    shift_ref[...] = jnp.zeros_like(shift_ref)
    for field in range(2):
        surface = surface_ref[field]
        pieces = [surface[row : row + 1, :] for row in range(surface.shape[0])]
        pieces.append(jnp.zeros((1, length - surface.size), jnp.float32))
        flat = jnp.concatenate(pieces, axis=1)
        for i in range(rows + 1):
            amount = (rows - i) * span_y
            shift_ref[i : i + 1, :] = pltpu.roll(flat, amount, 1) if amount else flat
        base = shift_ref[0:tall, :]
        for j in range(width):
            shift_ref[j * tall : (j + 1) * tall, :] = pltpu.roll(base, width - j, 1)
        shift_ref[width * tall : (width + 1) * tall, :] = base
        wide = product(shift_ref[...], table_ref[field], 0)
        for j in range(width + 1):
            for i in range(rows + 1):
                data_ref[field, i, j : j + 1, :] = wide[j * tall + i : j * tall + i + 1]
            if j < width:
                grad_ref[j * rows : (j + 1) * rows, :] = (
                    wide[j * tall : j * tall + rows] + force_ref[field, j]
                )
        spread_rows(
            project(grad_ref[...], table_ref[field]), out_ref, field, rows, width, span_y
        )


def parts_of(values):
    first = values.astype(jnp.bfloat16)
    rest = values - first.astype(jnp.float32)
    second = rest.astype(jnp.bfloat16)
    third = (rest - second.astype(jnp.float32)).astype(jnp.bfloat16)
    return jnp.concatenate([first, second, third], axis=0)


def hot_rows(indices, size, kind=jnp.float32):
    labels = lax.broadcasted_iota(jnp.int32, (size, indices.shape[1]), 0)
    return (labels == indices).astype(jnp.float32).astype(kind)


def leveller(lines):
    hot = hot_rows(lines, LINES, jnp.bfloat16)
    over = (((1,), (1,)), ((), ()))
    ones = jnp.ones((8, lines.shape[1]), jnp.bfloat16)
    counts = lax.dot_general(ones, hot, over, preferred_element_type=jnp.float32)[0:1]
    counts = jnp.maximum(counts, 1.0)

    def level(values):
        sums = lax.dot_general(parts_of(values), hot, over, preferred_element_type=jnp.float32)
        means = jnp.sum(sums, axis=0, keepdims=True) / counts
        spread = jnp.dot(parts_of(means), hot, preferred_element_type=jnp.float32)
        return values - jnp.sum(spread, axis=0, keepdims=True)

    return level


def places(cells, total_y, surface):
    hot_x = hot_rows(cells // total_y, surface.shape[0])
    hot_y = hot_rows(cells % total_y, surface.shape[1])
    return hot_x, hot_y


def at_stations(surface, hot_x, hot_y):
    count = surface.shape[0]
    parts = jnp.dot(
        parts_of(surface), hot_y.astype(jnp.bfloat16), preferred_element_type=jnp.float32
    )
    picked = parts[:count] + parts[count : 2 * count] + parts[2 * count :]
    return jnp.sum(picked * hot_x, axis=0, keepdims=True)


def to_surface(values, hot_x, hot_y):
    count = hot_x.shape[0]
    parts = lax.dot_general(
        parts_of(hot_x * values), hot_y.astype(jnp.bfloat16), (((1,), (1,)), ((), ())),
        preferred_element_type=jnp.float32,
    )
    return parts[:count] + parts[count : 2 * count] + parts[2 * count :]


def unpacked(flat_ref, field, chunks, surface_ref):
    pieces = [
        flat_ref[field * chunks + chunk : field * chunks + chunk + 1, :]
        for chunk in range(chunks)
    ]
    flat = jnp.concatenate(pieces, axis=1)
    rows, span_y = surface_ref.shape
    for row in range(rows):
        surface_ref[row : row + 1, :] = flat[:, row * span_y : (row + 1) * span_y]
    return surface_ref[...]


def source_kernel(total_y, surface_ref, packed_ref, weighted_ref, source_ref, hold_ref):
    for field in range(2):
        cells = packed_ref[field : field + 1, :].astype(jnp.int32)
        level = leveller(packed_ref[2 + field : 3 + field, :].astype(jnp.int32))
        weight = packed_ref[6 + field : 7 + field, :]
        surface = unpacked(surface_ref, field, surface_ref.shape[0] // 2, hold_ref)
        hot_x, hot_y = places(cells, total_y, surface)
        predicted = at_stations(surface, hot_x, hot_y)
        weighted = weight * level(predicted - packed_ref[4 + field : 5 + field, :])
        weighted_ref[field : field + 1, :] = weighted
        source = level(weight * weighted)
        source_ref[field] = to_surface(source, hot_x, hot_y)


def trial_kernel(total_y, coupling, total_ref, packed_ref, weighted_ref, step_ref, out_ref, hold_ref):
    chunks = total_ref.shape[0] // 2 - 4
    tail = total_ref[2 * chunks :, :]
    peak = jnp.max(tail[5:6, :], axis=1, keepdims=True) + 1e-06
    steps = step_ref[...]
    ratio = steps / peak
    energy = jnp.sum(tail[4:5, :], axis=1, keepdims=True)
    for order in (3, 2, 1, 0):
        energy = energy * ratio + jnp.sum(tail[order : order + 1, :], axis=1, keepdims=True)
    value = coupling * energy
    for field in range(2):
        cells = packed_ref[field : field + 1, :].astype(jnp.int32)
        level = leveller(packed_ref[2 + field : 3 + field, :].astype(jnp.int32))
        surface = unpacked(total_ref, field, chunks, hold_ref)
        hot_x, hot_y = places(cells, total_y, surface)
        image = at_stations(surface, hot_x, hot_y) / peak
        change = packed_ref[6 + field : 7 + field, :] * level(image)
        moved = weighted_ref[field : field + 1, :] - steps * change
        value = value + jnp.sum(moved * moved, axis=1, keepdims=True)
    stations = 2 * packed_ref.shape[1]
    count = value.shape[0]
    here = lax.broadcasted_iota(jnp.int32, (count, count), 0) == lax.broadcasted_iota(
        jnp.int32, (count, count), 1
    )
    out_ref[...] = jnp.sum(jnp.where(here, 0.5 * value / stations, 0.0), axis=0, keepdims=True)


def masks(rows, width, start_x, start_y, total_x, total_y):
    global_x = start_x + jnp.arange(rows, dtype=jnp.int32)
    global_y = start_y + jnp.arange(width, dtype=jnp.int32)
    mask_x = ((global_x >= 0) & (global_x < total_x - 1)).astype(jnp.float32)[:, None, None]
    mask_y = ((global_y >= 0) & (global_y < total_y - 1)).astype(jnp.float32)[None, :, None]
    valid = (global_x >= 0)[:, None] & (global_y >= 0)[None, :]
    valid = valid & (global_x < total_x)[:, None] & (global_y < total_y)[None, :]
    return (mask_x, mask_y, valid.astype(jnp.float32)[:, :, None])


def differences(field, mask_x, mask_y):
    base = field[:-1, :-1, :]
    along_x = (field[1:, :-1, :] - base) * mask_x
    along_y = (field[:-1, 1:, :] - base) * mask_y
    along_z = jnp.concatenate(
        [base[:, :, 1:] - base[:, :, :-1], jnp.zeros_like(base[:, :, :1])], axis=2
    )
    return (along_x, along_y, along_z)


def cross(a, b):
    return (
        a[1] * b[2] - a[2] * b[1],
        a[2] * b[0] - a[0] * b[2],
        a[0] * b[1] - a[1] * b[0],
    )


def inner(a, b):
    return a[0] * b[0] + a[1] * b[1] + a[2] * b[2]


def adjoint_differences(force, mask_x, mask_y):
    fx = force[0] * mask_x
    fy = force[1] * mask_y
    fz = force[2]
    keep = lax.broadcasted_iota(jnp.int32, fz.shape, 2) < fz.shape[2] - 1
    fz = jnp.where(keep, fz, 0.0)
    lower = jnp.concatenate([jnp.zeros_like(fz[:, :, :1]), fz[:, :, :-1]], axis=2)
    return (
        (fx[:-1, 1:] - fx[1:, 1:]) + (fy[1:, :-1] - fy[1:, 1:]) + (lower - fz)[1:, 1:]
    )


def from_all(values):
    count = lax.axis_size("gx") * lax.axis_size("gy")
    copies = jnp.broadcast_to(values[None], (count,) + values.shape)
    return lax.all_to_all(copies, ("gx", "gy"), 0, 0, tiled=True)


def everywhere(values):
    return jnp.sum(from_all(values), axis=0)


def doubled(values, largest):
    is_largest = lax.broadcasted_iota(jnp.int32, values.shape, 0) == largest
    for axis in ("gy", "gx"):
        count = lax.axis_size(axis)
        hop = 1
        while hop < count:
            other = lax.ppermute(values, axis, [(i, i ^ hop) for i in range(count)])
            values = jnp.where(is_largest, jnp.maximum(values, other), values + other)
            hop *= 2
    return values


def all_groups(values):
    groups = lax.axis_size("gx")
    group = lax.axis_index("gx")
    pieces = jnp.stack(
        [values]
        + [
            lax.ppermute(values, "gx", [(i, (i + hop) % groups) for i in range(groups)])
            for hop in range(1, groups)
        ]
    )
    return jnp.concatenate(
        [
            lax.dynamic_index_in_dim(pieces, (group - turn) % groups, 0, keepdims=False)
            for turn in range(groups)
        ],
        axis=1,
    )


def body(density, susceptibility, station_cell, station_line, observed, data_weight, trial_steps):
    rows, width, layers = density.shape
    groups = lax.axis_size("gx")
    columns = lax.axis_size("gy")
    total_x = rows * groups
    total_y = width * columns
    stations = station_cell.shape[1] * groups
    group = lax.axis_index("gx")
    anchor_x = group * rows
    anchor_y = lax.axis_index("gy") * width
    coupling = coupling_scale * stations / (total_x * total_y * layers)
    models = jnp.stack([density, susceptibility])

    packed = jnp.concatenate(
        [
            station_cell.astype(jnp.float32),
            station_line.astype(jnp.float32),
            observed,
            data_weight,
        ]
    )
    packed = all_groups(packed)
    span_y = -(-(total_y + width) // 8) * 8
    surface_shape = (2, total_x, span_y)
    sizes = (rows, width, span_y)
    length = -(-(total_x + rows) // 16) * 16 * span_y
    chunks = -(-total_x * span_y // 128)
    vmem = pl.BlockSpec(memory_space=pltpu.VMEM)
    surface_out = jax.ShapeDtypeStruct((2 * chunks, 128), jnp.float32)
    table_out = jax.ShapeDtypeStruct((2, length, layers), jnp.float32)
    wide_shape = (2, rows + 1, width + 1, layers)
    tall = -(-(rows + 1) // 8) * 8
    by_column = jnp.swapaxes(models, 1, 2).reshape(2, width * rows, layers)
    table, predicted = pl.pallas_call(
        functools.partial(first_kernel, sizes),
        in_specs=[pl.BlockSpec(memory_space=pltpu.SMEM), vmem],
        out_specs=(vmem, vmem),
        out_shape=(table_out, surface_out),
    )(jnp.stack([-rows - anchor_x, -width - anchor_y]), by_column)

    wide = extended(models, 1, 2)
    mask_x, mask_y, valid = masks(
        rows + 2, width + 2, anchor_x - 1, anchor_y - 1, total_x, total_y
    )
    a = differences(wide[0], mask_x, mask_y)
    b = differences(wide[1], mask_x, mask_y)
    t = tuple(part * valid for part in cross(a, b))
    pull_a = cross(b, t)
    pull_b = cross(t, a)
    force = jnp.stack(
        [
            adjoint_differences(pull_a, mask_x, mask_y),
            adjoint_differences(pull_b, mask_x, mask_y),
        ]
    )
    cross_force = force[:, :rows, :width]
    pulled = coupling * jnp.swapaxes(cross_force, 1, 2)

    weighted, surface = pl.pallas_call(
        functools.partial(source_kernel, total_y),
        in_specs=[vmem, vmem],
        out_specs=(vmem, vmem),
        out_shape=(
            jax.ShapeDtypeStruct((2, stations), jnp.float32),
            jax.ShapeDtypeStruct(surface_shape, jnp.float32),
        ),
        scratch_shapes=[pltpu.VMEM(surface_shape[1:], jnp.float32)],
    )(everywhere(predicted), packed)
    data_wide, image_part = pl.pallas_call(
        functools.partial(middle_kernel, sizes),
        in_specs=[vmem, vmem, vmem],
        out_specs=(vmem, vmem),
        out_shape=(jax.ShapeDtypeStruct(wide_shape, jnp.float32), surface_out),
        scratch_shapes=[
            pltpu.VMEM(((width + 1) * tall, length), jnp.float32),
            pltpu.VMEM((width * rows, layers), jnp.float32),
        ],
    )(surface, table, pulled)
    data_gradient = data_wide[:, :rows, :width]
    gradient_wide = data_wide + coupling * force
    gradient = gradient_wide[:, :rows, :width]

    own_a = tuple(part[1:-1, 1:-1] for part in a)
    own_b = tuple(part[1:-1, 1:-1] for part in b)
    own_t = tuple(part[1:-1, 1:-1] for part in t)
    own_mask = (mask_x[1:-1], mask_y[:, 1:-1])
    da = differences(gradient_wide[0], *own_mask)
    db = differences(gradient_wide[1], *own_mask)
    t1 = tuple(-(p + q) for p, q in zip(cross(da, own_b), cross(own_a, db)))
    t2 = cross(da, db)
    def lanes(values):
        return jnp.sum(values, axis=(0, 1))[None]

    tail = (
        lanes(inner(own_t, own_t)),
        lanes(2.0 * inner(own_t, t1)),
        lanes(inner(t1, t1) + 2.0 * inner(own_t, t2)),
        lanes(2.0 * inner(t1, t2)),
        lanes(inner(t2, t2)),
        jnp.max(jnp.abs(gradient), axis=(0, 1, 2))[None],
        jnp.zeros((2, layers), jnp.float32),
    )
    total = doubled(jnp.concatenate((image_part,) + tail), 2 * chunks + 5)
    trial_values = pl.pallas_call(
        functools.partial(trial_kernel, total_y, coupling),
        in_specs=[vmem] * 4,
        out_specs=vmem,
        out_shape=jax.ShapeDtypeStruct((1, trial_steps.shape[0]), jnp.float32),
        scratch_shapes=[pltpu.VMEM(surface_shape[1:], jnp.float32)],
    )(total, packed, weighted, trial_steps[:, None])
    trial_values = trial_values.reshape(-1)
    weighted_residual = lax.dynamic_slice_in_dim(
        weighted, group * station_cell.shape[1], station_cell.shape[1], 1
    )
    return (data_gradient, cross_force, weighted_residual, trial_values)


def solution(mesh):
    placed = (
        P("gx", "gy", None),
        P("gx", "gy", None),
        P(None, "gx"),
        P(None, "gx"),
        P(None, "gx"),
        P(None, "gx"),
        P(),
    )
    return jax.shard_map(
        body,
        mesh=mesh,
        in_specs=placed,
        out_specs=(P(None, "gx", "gy", None), P(None, "gx", "gy", None), P(None, "gx"), P()),
        check_vma=False,
    )
```
